32 devices in a mesh: seq: 8 (over z, x), tp: 4 (over y, core).
Axes of the slice: x: 2, y: 2, z: 4, core: 2. Of those that a mesh axis runs over, the one named last changes fastest.
Arguments:
- block_in: bfloat16 [2, 1024, 1024], P(None, 'seq', 'tp'), may hold values from -6 to 6
- out_grad: bfloat16 [2, 1024, 1024], P(None, 'seq', 'tp'), may hold values from -6 to 6
- decay_code: int32 [2, 1024, 8], P(None, 'seq', 'tp'), may hold values from 0 to 14
- beta_code: int32 [2, 1024, 8], P(None, 'seq', 'tp'), may hold values from 0 to 7
- norm_gain: bfloat16 [1024], P('seq'), may hold values from 0.5 to 1.5
- w_query: bfloat16 [1024, 1024], P('seq', 'tp'), may hold values from -0.1875 to 0.1875
- w_key: bfloat16 [1024, 1024], P('seq', 'tp'), may hold values from -0.1875 to 0.1875
- w_value: bfloat16 [1024, 2048], P('seq', 'tp'), may hold values from -0.1875 to 0.1875
- w_outgate: bfloat16 [1024, 2048], P('seq', 'tp'), may hold values from -0.1875 to 0.1875
- conv_query: bfloat16 [4, 8, 128], P(None, 'tp', 'seq'), may hold values from -3 to 3
- conv_key: bfloat16 [4, 8, 128], P(None, 'tp', 'seq'), may hold values from -3 to 3
- conv_value: bfloat16 [4, 8, 256], P(None, 'tp', 'seq'), may hold values from -3 to 3
- head_gain: bfloat16 [8, 256], P('tp', 'seq'), may hold values from 0.5 to 1.5
- w_output: bfloat16 [2048, 1024], P('tp', 'seq'), may hold values from -0.125 to 0.125
- mlp_gain: bfloat16 [1024], P('seq'), may hold values from 0.5 to 1.5
- w_gate: bfloat16 [1024, 2816], P('seq', 'tp'), may hold values from -0.1875 to 0.1875
- w_up: bfloat16 [1024, 2816], P('seq', 'tp'), may hold values from -0.1875 to 0.1875
- w_down: bfloat16 [2816, 1024], P('tp', 'seq'), may hold values from -0.109375 to 0.109375
Outputs:
- block_out: bfloat16 [2, 1024, 1024], P(None, 'seq', 'tp')
- grad_in: float32 [2, 1024, 1024], P(None, 'seq', 'tp')
- grad_norm_gain: float32 [1024], P('seq')
- grad_query: float32 [1024, 1024], P('seq', 'tp')
- grad_key: float32 [1024, 1024], P('seq', 'tp')
- grad_value: float32 [1024, 2048], P('seq', 'tp')
- grad_outgate: float32 [1024, 2048], P('seq', 'tp')
- grad_conv_query: float32 [4, 8, 128], P(None, 'tp', 'seq')
- grad_conv_key: float32 [4, 8, 128], P(None, 'tp', 'seq')
- grad_conv_value: float32 [4, 8, 256], P(None, 'tp', 'seq')
- grad_head_gain: float32 [8, 256], P('tp', 'seq')
- grad_output: float32 [2048, 1024], P('tp', 'seq')
- grad_mlp_gain: float32 [1024], P('seq')
- grad_gate: float32 [1024, 2816], P('seq', 'tp')
- grad_up: float32 [1024, 2816], P('seq', 'tp')
- grad_down: float32 [2816, 1024], P('tp', 'seq')
The draws below stay inside these ranges and needn't reach their ends.
All inputs are finite; a program needn't handle non-finite values.
Results may differ from the reference program's by a relative error of at most 0.019.
Values may be sent and summed in bfloat16 or wider, within the bound.
A program may use at most 128 MiB of HBM per device.

```python
import jax
import jax.numpy as jnp
from jax import lax

D = 1024
H = 8
DK = 128
DV = 256
FF = 2816
CONV = 4
BLOCK = 64
SEQS = 2
SEQUENCE_LENGTH = 1024
HK = 1024
HV = 2048


def draw_decay_code(key, part):
    ranking = jax.random.permutation(jax.random.fold_in(key, 12), H)
    base_level = 4 + ranking * 9 // (H - 1)
    offsets = jax.random.randint(jax.random.fold_in(key, 13), (SEQS, SEQUENCE_LENGTH, H), 0, 2)
    offsets = offsets.at[:, 0, :].set(1)
    quantized_levels = base_level[None, None, :] + offsets
    locations = jax.random.randint(jax.random.fold_in(key, 14), (SEQS, 6), 1, SEQUENCE_LENGTH)
    event_mask = jnp.any(jnp.arange(SEQUENCE_LENGTH)[None, :, None] == locations[:, None, :], axis=2)
    return jnp.where(event_mask[:, :, None], 0, quantized_levels).astype(jnp.int32)


def set_ends(entries, key, least, largest):
    index_at = [jax.random.randint(jax.random.fold_in(key, axis), (), 0, length) for axis, length in enumerate(entries.shape)]
    longest = entries.shape.index(max(entries.shape))
    next_to = index_at[:longest] + [(index_at[longest] + 1) % entries.shape[longest]] + index_at[longest + 1:]
    return entries.at[tuple(index_at)].set(least).at[tuple(next_to)].set(largest)


def strengthened(drawn, own_key, source, target, parts, factor):
    owner, partner = [(jnp.arange(drawn.shape[position]) // (drawn.shape[position] // parts)).reshape([-1 if axis == position else 1 for axis in range(drawn.ndim)]) for position in (source, target)]
    chosen = jax.random.permutation(own_key, parts)[partner]
    strong = (owner == chosen) | (owner == (partner + parts // 2) % parts)
    return jnp.where(strong, factor * drawn, drawn)


def shard_levels(rng, extent, cuts, low, top_value):
    def one(position, shards_of):
        draws = jax.random.uniform(jax.random.fold_in(jax.random.fold_in(rng, 6), position), (shards_of,), jnp.float32, low / len(cuts), top_value / len(cuts))
        return jnp.repeat(jnp.exp(draws), extent[position] // shards_of).reshape((-1,) + (1,) * (len(extent) - position - 1))

    factor_of = one(*cuts[0])
    for cut in cuts[1:]:
        factor_of = factor_of * one(*cut)
    return factor_of


def noise(stream_key, dims, scale, most, cuts=(), kind=jnp.bfloat16):
    factor_of = shard_levels(stream_key, dims, cuts, -0.22, 0.18) if cuts else 1.0
    values = jax.random.normal(stream_key, dims, jnp.float32) * scale * factor_of
    return jnp.minimum(jnp.maximum(values, -most), most).astype(kind)


def gaussian_with(stream_key, extent, deviation, limit, cuts, heavy, held_as=jnp.bfloat16):
    array = deviation * jax.random.normal(stream_key, extent, jnp.float32)
    if cuts:
        array = array * shard_levels(stream_key, extent, cuts, -0.22, 0.18)
    return jnp.clip(strengthened(array, jax.random.fold_in(stream_key, 3), *heavy), -limit, limit).astype(held_as)


def setup_inputs(seed: int = 0) -> dict:
    streams_of = jax.random.split(jax.random.key(seed), 19)
    block_in = gaussian_with(streams_of[0], (SEQS, SEQUENCE_LENGTH, D), 1.0, 6.0, ((1, 8), (2, 4)), (1, 2, 8, 2.0))
    out_grad = gaussian_with(streams_of[1], (SEQS, SEQUENCE_LENGTH, D), 1.0, 6.0, ((1, 8), (2, 4)), (1, 2, 8, 2.0))
    decay_code = draw_decay_code(jax.random.fold_in(streams_of[18], 71), 0)
    beta_code = set_ends(jax.random.randint(streams_of[3], (SEQS, SEQUENCE_LENGTH, H), 0, 8), jax.random.fold_in(streams_of[3], 1), 0, 7).astype(jnp.int32)
    norm_gain = jnp.clip(1.0 + 0.1 * jax.random.normal(streams_of[4], (D,), jnp.float32), 0.5, 1.5).astype(jnp.bfloat16)
    w_query = noise(streams_of[5], (D, HK), D ** -0.5, 0.1875, ((0, 8), (1, 4)))
    w_key = noise(streams_of[6], (D, HK), D ** -0.5, 0.1875, ((0, 8), (1, 4)))
    w_value = noise(streams_of[7], (D, HV), D ** -0.5, 0.1875, ((0, 8), (1, 4)))
    w_outgate = noise(streams_of[8], (D, HV), D ** -0.5, 0.1875, ((0, 8), (1, 4)))
    conv_query = noise(streams_of[9], (CONV, H, DK), CONV ** -0.5, 3.0, ((1, 4), (2, 8)))
    conv_key = noise(streams_of[10], (CONV, H, DK), CONV ** -0.5, 3.0, ((1, 4), (2, 8)))
    conv_value = noise(streams_of[11], (CONV, H, DV), CONV ** -0.5, 3.0, ((1, 4), (2, 8)))
    head_gain = jnp.clip(1.0 + 0.1 * jax.random.normal(streams_of[12], (H, DV), jnp.float32), 0.5, 1.5).astype(jnp.bfloat16)
    w_output = noise(streams_of[13], (HV, D), HV ** -0.5, 0.125, ((0, 4), (1, 8)))
    mlp_gain = jnp.clip(1.0 + 0.1 * jax.random.normal(streams_of[14], (D,), jnp.float32), 0.5, 1.5).astype(jnp.bfloat16)
    w_gate = noise(streams_of[15], (D, FF), D ** -0.5, 0.1875, ((0, 8), (1, 4)))
    w_up = noise(streams_of[16], (D, FF), D ** -0.5, 0.1875, ((0, 8), (1, 4)))
    w_down = noise(streams_of[17], (FF, D), FF ** -0.5, 0.109375, ((0, 4), (1, 8)))
    return {"block_in": block_in, "out_grad": out_grad, "decay_code": decay_code, "beta_code": beta_code, "norm_gain": norm_gain, "w_query": w_query, "w_key": w_key, "w_value": w_value, "w_outgate": w_outgate, "conv_query": conv_query, "conv_key": conv_key, "conv_value": conv_value, "head_gain": head_gain, "w_output": w_output, "mlp_gain": mlp_gain, "w_gate": w_gate, "w_up": w_up, "w_down": w_down}


PRECISE = lax.Precision.HIGHEST
EPSILON = 1e-06
LOG_TWO = 0.6931471805599453

def row_scale(values):
    return lax.rsqrt(lax.optimization_barrier(jnp.mean(values * values, axis=-1, keepdims=True)) + EPSILON)

def silu_slope(values):
    sigmoid = jax.nn.sigmoid(values)
    return sigmoid * (1.0 + values * (1.0 - sigmoid))

def norm_back(d_normed, inputs, scales, gains):
    weighted = d_normed * gains
    return scales * (weighted - inputs * scales * scales * lax.optimization_barrier(jnp.mean(weighted * inputs, axis=-1, keepdims=True)))

def unit_inverse(strict_part):
    width = strict_part.shape[-1]
    negated = -strict_part
    result = jnp.eye(width, dtype=strict_part.dtype) + negated
    for rounds in range(width.bit_length() - 2):
        negated = jnp.matmul(negated, negated, precision=PRECISE)
        result = result + jnp.matmul(result, negated, precision=PRECISE)
    return result

def group_step(state_in, query, keys, values, log_decay, write_strength_rate):
    width = log_decay.shape[-1]
    cumulative = jnp.cumsum(log_decay, axis=-1)
    locations = jnp.arange(width)
    strictly = (locations[:, None] > locations[None, :]).astype(state_in.dtype)
    up_to = locations[:, None] >= locations[None, :]
    spread = cumulative[..., :, None] - cumulative[..., None, :]
    factors = jnp.exp(jnp.where(up_to, spread, 0.0)) * up_to.astype(state_in.dtype)
    key_dots = jnp.einsum('...td,...sd->...ts', keys, keys, precision=PRECISE)
    inverse = unit_inverse(write_strength_rate[..., :, None] * key_dots * factors * strictly)
    growth = jnp.exp(cumulative)
    targets = write_strength_rate[..., None] * (values - growth[..., None] * jnp.einsum('...td,...dw->...tw', keys, state_in, precision=PRECISE))
    update = jnp.matmul(inverse, targets, precision=PRECISE)
    scores = jnp.einsum('...td,...sd->...ts', query, keys, precision=PRECISE) * factors
    output = growth[..., None] * jnp.einsum('...td,...dw->...tw', query, state_in, precision=PRECISE) + jnp.matmul(scores, update, precision=PRECISE)
    final_log = cumulative[..., -1:]
    carried = jnp.exp(final_log)[..., None] * state_in + jnp.einsum('...sd,...sw->...dw', keys * jnp.exp(final_log - cumulative)[..., None], update, precision=PRECISE)
    return (carried, output)

def delta_run(state_in, query, keys, values, log_decay, write_strength_rate):
    leading = query.shape[:-2]
    length = query.shape[-2]
    blocks = length // BLOCK
    axis_at = len(leading)

    def split_blocks(tensor):
        tensor = tensor.reshape(leading + (blocks, BLOCK) + tensor.shape[axis_at + 1:])
        return jnp.moveaxis(tensor, axis_at, 0)

    def advance(carried, pieces):
        return jax.checkpoint(group_step)(carried, *pieces)
    end_state, outputs = lax.scan(advance, state_in, (split_blocks(query), split_blocks(keys), split_blocks(values), split_blocks(log_decay), split_blocks(write_strength_rate)))
    outputs = jnp.moveaxis(outputs, 0, axis_at)
    return (outputs.reshape(leading + (length, outputs.shape[-1])), end_state)

def conv_valid(kernel, extended):
    length = extended.shape[1] - kernel.shape[0] + 1
    return sum((kernel[offset] * extended[:, offset:offset + length] for offset in range(kernel.shape[0])))

def heads_first(tensor, width):
    shaped = tensor.reshape(tensor.shape[0], tensor.shape[1], -1, width)
    return jnp.transpose(shaped, (0, 2, 1, 3))

def rows_last(tensor):
    shaped = jnp.transpose(tensor, (0, 2, 1, 3))
    return shaped.reshape(shaped.shape[0], shaped.shape[1], -1)

def activate(kern_query, kern_key, kern_value, ext_query, ext_key, ext_value):
    query = heads_first(jax.nn.silu(conv_valid(kern_query, ext_query)), DK)
    query = query * lax.rsqrt(lax.optimization_barrier(jnp.sum(query * query, axis=-1, keepdims=True)) + EPSILON) * DK ** (-0.5)
    keys = heads_first(jax.nn.silu(conv_valid(kern_key, ext_key)), DK)
    keys = keys * lax.rsqrt(lax.optimization_barrier(jnp.sum(keys * keys, axis=-1, keepdims=True)) + EPSILON)
    values = heads_first(jax.nn.silu(conv_valid(kern_value, ext_value)), DV)
    return (query, keys, values)

def gate_rates(decay_code, beta_code):
    log_decay = -0.5 * jnp.exp(-LOG_TWO * decay_code.astype(jnp.float32))
    write_strength_rate = (beta_code.astype(jnp.float32) + 1.0) / 8.0
    return (jnp.moveaxis(log_decay, 2, 1), jnp.moveaxis(write_strength_rate, 2, 1))

def reference(block_in, out_grad, decay_code, beta_code, norm_gain, w_query, w_key, w_value, w_outgate, conv_query, conv_key, conv_value, head_gain, w_output, mlp_gain, w_gate, w_up, w_down):
    residual = block_in.astype(jnp.float32).reshape(-1, D)
    scale_one = row_scale(residual)
    gain_one = norm_gain.astype(jnp.float32)
    normed = (residual * scale_one * gain_one).astype(jnp.bfloat16)
    proj_query = jnp.dot(normed, w_query, preferred_element_type=jnp.float32)
    proj_key = jnp.dot(normed, w_key, preferred_element_type=jnp.float32)
    proj_value = jnp.dot(normed, w_value, preferred_element_type=jnp.float32)
    proj_outgate = jnp.dot(normed, w_outgate, preferred_element_type=jnp.float32)

    def extend(tensor):
        return jnp.pad(tensor.reshape(SEQS, SEQUENCE_LENGTH, -1), ((0, 0), (CONV - 1, 0), (0, 0)))
    kernels = tuple((kernel.astype(jnp.float32).reshape(CONV, -1) for kernel in (conv_query, conv_key, conv_value)))
    extended = (extend(proj_query), extend(proj_key), extend(proj_value))
    log_decay, write_strength_rate = gate_rates(decay_code, beta_code)
    start_zero = jnp.zeros((SEQS, H, DK, DV), jnp.float32)

    def mixer(kern_query, kern_key, kern_value, ext_query, ext_key, ext_value):
        query, keys, values = activate(kern_query, kern_key, kern_value, ext_query, ext_key, ext_value)
        return delta_run(start_zero, query, keys, values, log_decay, write_strength_rate)[0]
    mixed, mixer_back = jax.vjp(mixer, kernels[0], kernels[1], kernels[2], extended[0], extended[1], extended[2])
    head_scale = row_scale(mixed)
    gain_head = head_gain.astype(jnp.float32)[None, :, None, :]
    head_out = mixed * head_scale * gain_head
    gate_pre = heads_first(proj_outgate.reshape(SEQS, SEQUENCE_LENGTH, -1), DV)
    gated = rows_last(head_out * jax.nn.silu(gate_pre)).reshape(-1, HV).astype(jnp.bfloat16)
    middle = residual + jnp.dot(gated, w_output, preferred_element_type=jnp.float32)
    scale_two = row_scale(middle)
    gain_two = mlp_gain.astype(jnp.float32)
    normed_two = (middle * scale_two * gain_two).astype(jnp.bfloat16)
    pre_gate = jnp.dot(normed_two, w_gate, preferred_element_type=jnp.float32)
    pre_up = jnp.dot(normed_two, w_up, preferred_element_type=jnp.float32)
    hidden = (jax.nn.silu(pre_gate) * pre_up).astype(jnp.bfloat16)
    block_out = (middle + jnp.dot(hidden, w_down, preferred_element_type=jnp.float32)).astype(jnp.bfloat16)
    cotangent = out_grad.reshape(-1, D)
    d_hidden = jnp.dot(cotangent, w_down.T, preferred_element_type=jnp.float32)
    grad_down = jnp.dot(hidden.T, cotangent, preferred_element_type=jnp.float32)
    d_pre_gate = (d_hidden * pre_up * silu_slope(pre_gate)).astype(jnp.bfloat16)
    d_pre_up = (d_hidden * jax.nn.silu(pre_gate)).astype(jnp.bfloat16)
    d_normed_two = jnp.dot(d_pre_gate, w_gate.T, preferred_element_type=jnp.float32) + jnp.dot(d_pre_up, w_up.T, preferred_element_type=jnp.float32)
    grad_gate = jnp.dot(normed_two.T, d_pre_gate, preferred_element_type=jnp.float32)
    grad_up = jnp.dot(normed_two.T, d_pre_up, preferred_element_type=jnp.float32)
    grad_mlp_gain = lax.optimization_barrier(jnp.sum(d_normed_two * middle * scale_two, axis=0))
    d_middle = cotangent.astype(jnp.float32) + norm_back(d_normed_two, middle, scale_two, gain_two)
    d_mid_low = d_middle.astype(jnp.bfloat16)
    d_gated = jnp.dot(d_mid_low, w_output.T, preferred_element_type=jnp.float32)
    grad_output = jnp.dot(gated.T, d_mid_low, preferred_element_type=jnp.float32)
    d_gated_heads = heads_first(d_gated.reshape(SEQS, SEQUENCE_LENGTH, -1), DV)
    d_outgate = rows_last(d_gated_heads * head_out * silu_slope(gate_pre)).reshape(-1, HV).astype(jnp.bfloat16)
    d_head = d_gated_heads * jax.nn.silu(gate_pre)
    grad_head_gain = lax.optimization_barrier(jnp.sum(d_head * mixed * head_scale, axis=(0, 2)))
    d_mixed = norm_back(d_head, mixed, head_scale, gain_head)
    mixer_grads = mixer_back(d_mixed)
    d_proj_query = mixer_grads[3][:, CONV - 1:].reshape(-1, HK).astype(jnp.bfloat16)
    d_proj_key = mixer_grads[4][:, CONV - 1:].reshape(-1, HK).astype(jnp.bfloat16)
    d_proj_value = mixer_grads[5][:, CONV - 1:].reshape(-1, HV).astype(jnp.bfloat16)
    d_normed = jnp.dot(d_proj_query, w_query.T, preferred_element_type=jnp.float32)
    d_normed = d_normed + jnp.dot(d_proj_key, w_key.T, preferred_element_type=jnp.float32)
    d_normed = d_normed + jnp.dot(d_proj_value, w_value.T, preferred_element_type=jnp.float32)
    d_normed = d_normed + jnp.dot(d_outgate, w_outgate.T, preferred_element_type=jnp.float32)
    grad_query = jnp.dot(normed.T, d_proj_query, preferred_element_type=jnp.float32)
    grad_key = jnp.dot(normed.T, d_proj_key, preferred_element_type=jnp.float32)
    grad_value = jnp.dot(normed.T, d_proj_value, preferred_element_type=jnp.float32)
    grad_outgate = jnp.dot(normed.T, d_outgate, preferred_element_type=jnp.float32)
    grad_norm_gain = lax.optimization_barrier(jnp.sum(d_normed * residual * scale_one, axis=0))
    grad_in = d_middle + norm_back(d_normed, residual, scale_one, gain_one)
    return (block_out.reshape(SEQS, SEQUENCE_LENGTH, D), grad_in.reshape(SEQS, SEQUENCE_LENGTH, D), grad_norm_gain, grad_query, grad_key, grad_value, grad_outgate, mixer_grads[0].reshape(CONV, H, DK), mixer_grads[1].reshape(CONV, H, DK), mixer_grads[2].reshape(CONV, H, DV), grad_head_gain, grad_output, grad_mlp_gain, grad_gate, grad_up, grad_down)
```

```python
import jax
import jax.numpy as jnp
from jax import lax
from jax.sharding import PartitionSpec as P

D = 1024
DK = 128
DV = 256
CONV = 4
BLOCK = 64


PRECISE = lax.Precision.HIGHEST
EPSILON = 1e-06
LOG_TWO = 0.6931471805599453


def shifted(block, axis, distance):
    devices = range(lax.axis_size(axis))
    route = [(i - distance, i) for i in devices if i - distance in devices]
    return lax.ppermute(block, axis, route)


def before_me(joint, axis):
    size = lax.axis_size(axis)
    held = shifted(joint.astype(jnp.bfloat16), axis, 1).astype(jnp.float32)
    distance = 1
    while distance < size:
        last = 2 * distance >= size
        sent = held[..., DK:] if last else held
        got = shifted(sent.astype(jnp.bfloat16), axis, distance).astype(jnp.float32)
        moved = jnp.matmul(held[..., :DK], got, precision=PRECISE)
        if last:
            return held[..., DK:] + moved
        held = jnp.concatenate(
            [moved[..., :DK], held[..., DK:] + moved[..., DK:]], axis=-1
        )
        distance *= 2
    return held[..., DK:]


def later_maps(transition, axis):
    size = lax.axis_size(axis)
    held = shifted(transition.astype(jnp.bfloat16), axis, -1).astype(jnp.float32)
    maps = [held]
    distance = 1
    while 2 * distance < size:
        got = shifted(held.astype(jnp.bfloat16), axis, -distance).astype(jnp.float32)
        held = jnp.matmul(got, held, precision=PRECISE)
        maps.append(held)
        distance *= 2
    return maps


def after_me(d_start, maps, axis):
    size = lax.axis_size(axis)
    held = shifted(d_start.astype(jnp.bfloat16), axis, -1).astype(jnp.float32)
    distance = 1
    for step in maps:
        if distance >= size:
            break
        got = shifted(held.astype(jnp.bfloat16), axis, -distance).astype(jnp.float32)
        held = held + jnp.einsum("bhkj,bhkw->bhjw", step, got, precision=PRECISE)
        distance *= 2
    return held


def row_scale(values):
    return lax.rsqrt(jnp.mean(values * values, axis=-1, keepdims=True) + EPSILON)


def silu_slope(values):
    sigmoid = jax.nn.sigmoid(values)
    return sigmoid * (1.0 + values * (1.0 - sigmoid))


def norm_back(d_normed, inputs, scales, gains):
    weighted = d_normed * gains
    return scales * (
        weighted - inputs * scales * scales * jnp.mean(weighted * inputs, axis=-1, keepdims=True)
    )


def unit_inverse(strict_part):
    width = strict_part.shape[-1]
    negated = -strict_part
    result = jnp.eye(width, dtype=strict_part.dtype) + negated
    for rounds in range(width.bit_length() - 2):
        negated = jnp.matmul(negated, negated, precision=PRECISE)
        result = result + jnp.matmul(result, negated, precision=PRECISE)
    return result


def group_step(state_in, query, keys, values, log_decay, write_strength_rate):
    width = log_decay.shape[-1]
    cumulative = jnp.cumsum(log_decay, axis=-1)
    locations = jnp.arange(width)
    strictly = (locations[:, None] > locations[None, :]).astype(state_in.dtype)
    up_to = locations[:, None] >= locations[None, :]
    spread = cumulative[..., :, None] - cumulative[..., None, :]
    factors = jnp.exp(jnp.where(up_to, spread, 0.0)) * up_to.astype(state_in.dtype)
    key_dots = jnp.einsum("...td,...sd->...ts", keys, keys, precision=PRECISE)
    inverse = unit_inverse(write_strength_rate[..., :, None] * key_dots * factors * strictly)
    growth = jnp.exp(cumulative)
    targets = write_strength_rate[..., None] * (
        values
        - growth[..., None] * jnp.einsum("...td,...dw->...tw", keys, state_in, precision=PRECISE)
    )
    update = jnp.matmul(inverse, targets, precision=PRECISE)
    scores = jnp.einsum("...td,...sd->...ts", query, keys, precision=PRECISE) * factors
    output = growth[..., None] * jnp.einsum(
        "...td,...dw->...tw", query, state_in, precision=PRECISE
    ) + jnp.matmul(scores, update, precision=PRECISE)
    final_log = cumulative[..., -1:]
    carried = jnp.exp(final_log)[..., None] * state_in + jnp.einsum(
        "...sd,...sw->...dw",
        keys * jnp.exp(final_log - cumulative)[..., None],
        update,
        precision=PRECISE,
    )
    return (carried, output)


def delta_run(state_in, query, keys, values, log_decay, write_strength_rate):
    leading = query.shape[:-2]
    length = query.shape[-2]
    blocks = length // BLOCK
    axis_at = len(leading)

    def split_blocks(tensor):
        tensor = tensor.reshape(leading + (blocks, BLOCK) + tensor.shape[axis_at + 1 :])
        return jnp.moveaxis(tensor, axis_at, 0)

    def advance(carried, pieces):
        return jax.checkpoint(group_step)(carried, *pieces)

    end_state, outputs = lax.scan(
        advance,
        state_in,
        (
            split_blocks(query),
            split_blocks(keys),
            split_blocks(values),
            split_blocks(log_decay),
            split_blocks(write_strength_rate),
        ),
    )
    outputs = jnp.moveaxis(outputs, 0, axis_at)
    return (outputs.reshape(leading + (length, outputs.shape[-1])), end_state)


def conv_valid(kernel, extended):
    length = extended.shape[1] - kernel.shape[0] + 1
    return sum(
        (
            kernel[offset] * extended[:, offset : offset + length]
            for offset in range(kernel.shape[0])
        )
    )


def heads_first(tensor, width):
    shaped = tensor.reshape(tensor.shape[0], tensor.shape[1], -1, width)
    return jnp.transpose(shaped, (0, 2, 1, 3))


def rows_last(tensor):
    shaped = jnp.transpose(tensor, (0, 2, 1, 3))
    return shaped.reshape(shaped.shape[0], shaped.shape[1], -1)


def activate(kern_query, kern_key, kern_value, ext_query, ext_key, ext_value):
    query = heads_first(jax.nn.silu(conv_valid(kern_query, ext_query)), DK)
    query = (
        query * lax.rsqrt(jnp.sum(query * query, axis=-1, keepdims=True) + EPSILON) * DK ** (-0.5)
    )
    keys = heads_first(jax.nn.silu(conv_valid(kern_key, ext_key)), DK)
    keys = keys * lax.rsqrt(jnp.sum(keys * keys, axis=-1, keepdims=True) + EPSILON)
    values = heads_first(jax.nn.silu(conv_valid(kern_value, ext_value)), DV)
    return (query, keys, values)


def gate_rates(decay_code, beta_code):
    log_decay = -0.5 * jnp.exp(-LOG_TWO * decay_code.astype(jnp.float32))
    write_strength_rate = (beta_code.astype(jnp.float32) + 1.0) / 8.0
    return (jnp.moveaxis(log_decay, 2, 1), jnp.moveaxis(write_strength_rate, 2, 1))


def fold_edge(tensor, incoming):
    margin = incoming.shape[1]
    return jnp.concatenate([tensor[:, :-margin], tensor[:, -margin:] + incoming], axis=1)


def per_device(
    block_in,
    out_grad,
    decay_code,
    beta_code,
    norm_gain,
    w_query,
    w_key,
    w_value,
    w_outgate,
    conv_query,
    conv_key,
    conv_value,
    head_gain,
    w_output,
    mlp_gain,
    w_gate,
    w_up,
    w_down,
):
    seq_count, tok_count, width_part = block_in.shape
    heads_here = decay_code.shape[2]
    ranks = lax.axis_size("seq")
    smalls = (norm_gain, mlp_gain, conv_query, conv_key, conv_value, head_gain)
    flat = jnp.concatenate([a.reshape(-1) for a in smalls])
    extra = -(-flat.shape[0] // norm_gain.shape[0])
    flat = jnp.pad(flat, (0, extra * norm_gain.shape[0] - flat.shape[0]))
    first = jnp.concatenate(
        [w_query, w_key, w_value, w_outgate, flat.reshape(norm_gain.shape[0], extra)], axis=1
    )
    widths = (w_query.shape[1], w_key.shape[1], w_value.shape[1], w_outgate.shape[1])
    mixer_width = sum(widths)
    first = lax.all_gather(first, "seq", axis=0, tiled=True)
    second = lax.all_gather(
        jnp.concatenate([w_gate, w_up, w_output.T, w_down.T], axis=1), "seq", axis=0, tiled=True
    )
    hidden_width = w_gate.shape[1]
    out_width = w_output.shape[0]
    full_mixer = first[:, :mixer_width]
    full_gate_up = second[:, : 2 * hidden_width]
    output_t = second[:, 2 * hidden_width : 2 * hidden_width + out_width]
    down_t = second[:, 2 * hidden_width + out_width :]
    gathered = first[:, mixer_width:].reshape(ranks, -1)
    parts, at = [], 0
    for a in smalls:
        parts.append(gathered[:, at : at + a.size].reshape((ranks,) + a.shape))
        at += a.size
    gain_one, gain_two = parts[0].reshape(-1), parts[1].reshape(-1)
    kern_query, kern_key, kern_value = (
        jnp.moveaxis(a, 0, 2).reshape(a.shape[1], a.shape[2], -1) for a in parts[2:5]
    )
    gain_head = jnp.moveaxis(parts[5], 0, 1).reshape(head_gain.shape[0], -1)
    gain_one = gain_one.astype(jnp.float32)
    gain_two = gain_two.astype(jnp.float32)
    gain_head = gain_head.astype(jnp.float32)[None, :, None, :]
    kernels = tuple(
        (
            kernel.astype(jnp.float32).reshape(CONV, -1)
            for kernel in (kern_query, kern_key, kern_value)
        )
    )
    input_full = lax.all_gather(block_in, "tp", axis=2, tiled=True)
    residual = input_full.astype(jnp.float32).reshape(-1, D)
    scale_one = row_scale(residual)
    normed = (residual * scale_one * gain_one).astype(jnp.bfloat16)
    projected = jnp.dot(normed, full_mixer, preferred_element_type=jnp.float32)
    cuts = (widths[0], widths[0] + widths[1], widths[0] + widths[1] + widths[2])
    proj_qkv = projected[:, : cuts[2]].reshape(seq_count, tok_count, -1)
    proj_outgate = projected[:, cuts[2] :]
    margin = CONV - 1
    before = shifted(proj_qkv[:, -margin:], "seq", 1)
    ext_qkv = jnp.concatenate([before, proj_qkv], axis=1)
    ext_query, ext_key, ext_value = (
        ext_qkv[..., : cuts[0]],
        ext_qkv[..., cuts[0] : cuts[1]],
        ext_qkv[..., cuts[1] :],
    )
    log_decay, write_strength_rate = gate_rates(decay_code, beta_code)
    eye_batch = jnp.broadcast_to(jnp.eye(DK, dtype=jnp.float32), (seq_count, heads_here, DK, DK))
    zero_state = jnp.zeros((seq_count, heads_here, DK, DV), jnp.float32)
    query, keys, values = activate(
        kernels[0], kernels[1], kernels[2], ext_query, ext_key, ext_value
    )
    start_joint = jnp.concatenate([eye_batch, zero_state], axis=-1)
    values_joint = jnp.concatenate(
        [jnp.zeros(values.shape[:-1] + (DK,), jnp.float32), values], axis=-1
    )
    out_joint, end_joint = delta_run(
        start_joint, query, keys, values_joint, log_decay, write_strength_rate
    )
    transition = end_joint[..., :DK]
    start_state = before_me(end_joint, "seq")
    maps = later_maps(transition, "seq")
    start_map = out_joint[..., :DK]
    mixed = out_joint[..., DK:] + jnp.einsum(
        "bhtk,bhkw->bhtw", start_map, start_state, precision=PRECISE
    )
    head_scale = row_scale(mixed)
    head_out = mixed * head_scale * gain_head
    gate_pre = heads_first(proj_outgate.reshape(seq_count, tok_count, -1), DV)
    gated = (
        rows_last(head_out * jax.nn.silu(gate_pre))
        .reshape(seq_count * tok_count, -1)
        .astype(jnp.bfloat16)
    )
    attn_part = jnp.einsum("tk,nk->tn", gated, output_t, preferred_element_type=jnp.float32)
    attn = lax.psum(attn_part.astype(jnp.bfloat16), "tp").astype(jnp.float32)
    middle = residual + attn
    tp_at = lax.axis_index("tp") * width_part
    mid_part = lax.dynamic_slice_in_dim(middle, tp_at, width_part, 1).reshape(
        seq_count, tok_count, width_part
    )
    scale_two = row_scale(middle)
    normed_two = (middle * scale_two * gain_two).astype(jnp.bfloat16)
    pre_both = jnp.dot(normed_two, full_gate_up, preferred_element_type=jnp.float32)
    pre_gate, pre_up = pre_both[:, :hidden_width], pre_both[:, hidden_width:]
    hidden = (jax.nn.silu(pre_gate) * pre_up).astype(jnp.bfloat16)
    feedforward_portion = jnp.einsum(
        "tk,nk->tn", hidden, down_t, preferred_element_type=jnp.float32
    ).reshape(seq_count, tok_count, D)
    block_out = (
        mid_part
        + lax.psum_scatter(
            feedforward_portion.astype(jnp.bfloat16), "tp", scatter_dimension=2, tiled=True
        ).astype(jnp.float32)
    ).astype(jnp.bfloat16)
    cot_full = lax.all_gather(out_grad, "tp", axis=2, tiled=True)
    cotangent = cot_full.reshape(-1, D)
    d_hidden = jnp.dot(cotangent, down_t, preferred_element_type=jnp.float32)
    grad_down_t = jnp.dot(cotangent.T, hidden, preferred_element_type=jnp.float32)
    d_pre_gate = (d_hidden * pre_up * silu_slope(pre_gate)).astype(jnp.bfloat16)
    d_pre_up = (d_hidden * jax.nn.silu(pre_gate)).astype(jnp.bfloat16)
    d_pre_both = jnp.concatenate([d_pre_gate, d_pre_up], axis=1)
    d_two_part = jnp.einsum(
        "tk,nk->tn", d_pre_both, full_gate_up, preferred_element_type=jnp.float32
    )
    d_normed_two = lax.psum(d_two_part.astype(jnp.bfloat16), "tp").astype(jnp.float32)
    grad_gate_up = jnp.dot(normed_two.T, d_pre_both, preferred_element_type=jnp.float32)
    grad_mlp_gain = jnp.sum(d_normed_two * middle * scale_two, axis=0)
    d_middle = cotangent.astype(jnp.float32) + norm_back(d_normed_two, middle, scale_two, gain_two)
    d_mid_low = d_middle.astype(jnp.bfloat16)
    d_gated = jnp.dot(d_mid_low, output_t, preferred_element_type=jnp.float32)
    grad_output_t = jnp.dot(d_mid_low.T, gated, preferred_element_type=jnp.float32)
    late = lax.psum_scatter(
        jnp.concatenate(
            [
                grad_gate_up.astype(jnp.bfloat16),
                grad_output_t.astype(jnp.bfloat16),
                grad_down_t.astype(jnp.bfloat16),
            ],
            axis=1,
        ),
        "seq",
        scatter_dimension=0,
        tiled=True,
    ).astype(jnp.float32)
    d_gated_heads = heads_first(d_gated.reshape(seq_count, tok_count, -1), DV)
    d_outgate = (
        rows_last(d_gated_heads * head_out * silu_slope(gate_pre))
        .reshape(seq_count * tok_count, -1)
        .astype(jnp.bfloat16)
    )
    d_head = d_gated_heads * jax.nn.silu(gate_pre)
    grad_head_gain = jnp.sum(d_head * mixed * head_scale, axis=(0, 2))
    d_mixed = norm_back(d_head, mixed, head_scale, gain_head)
    d_start = jnp.einsum("bhtk,bhtw->bhkw", start_map, d_mixed, precision=PRECISE)
    d_end = after_me(d_start, maps, "seq")

    def mixer(kern_q, kern_k, kern_v, ext_q, ext_k, ext_v, start_in):
        query_in, keys_in, values_in = activate(kern_q, kern_k, kern_v, ext_q, ext_k, ext_v)
        return delta_run(start_in, query_in, keys_in, values_in, log_decay, write_strength_rate)

    mixer_out, mixer_back = jax.vjp(
        mixer, kernels[0], kernels[1], kernels[2], ext_query, ext_key, ext_value, start_state
    )
    totals = mixer_back((d_mixed, d_end))
    d_ext = jnp.concatenate([totals[3], totals[4], totals[5]], axis=-1)
    after = shifted(d_ext[:, :margin], "seq", -1)
    d_proj = fold_edge(d_ext[:, margin:], after).reshape(seq_count * tok_count, -1)
    d_proj = jnp.concatenate([d_proj.astype(jnp.bfloat16), d_outgate], axis=1)
    d_normed_part = jnp.einsum("tk,nk->tn", d_proj, full_mixer, preferred_element_type=jnp.float32)
    grad_mixer = jnp.dot(normed.T, d_proj, preferred_element_type=jnp.float32)
    d_normed = (
        lax.psum(d_normed_part.reshape(seq_count, tok_count, D).astype(jnp.bfloat16), "tp")
        .astype(jnp.float32)
        .reshape(-1, D)
    )
    grad_norm_gain = jnp.sum(d_normed * residual * scale_one, axis=0)
    grad_full = (d_middle + norm_back(d_normed, residual, scale_one, gain_one)).reshape(
        seq_count, tok_count, D
    )
    grad_in = lax.dynamic_slice_in_dim(grad_full, lax.axis_index("tp") * width_part, width_part, 2)
    conv_grads = tuple(
        jnp.moveaxis(total.reshape(CONV, heads_here, ranks, -1), 2, 0).reshape(ranks, -1)
        for total in totals[:3]
    )
    small_grads = jnp.concatenate(
        [
            grad_norm_gain.reshape(ranks, -1),
            grad_mlp_gain.reshape(ranks, -1),
            *conv_grads,
            jnp.moveaxis(grad_head_gain.reshape(heads_here, ranks, -1), 1, 0).reshape(ranks, -1),
        ],
        axis=1,
    )
    small_grads = jnp.pad(
        small_grads, ((0, 0), (0, extra * norm_gain.shape[0] - small_grads.shape[1]))
    ).reshape(ranks * norm_gain.shape[0], extra)
    final = lax.psum_scatter(
        jnp.concatenate(
            [grad_mixer.astype(jnp.bfloat16), small_grads.astype(jnp.bfloat16)], axis=1
        ),
        "seq",
        scatter_dimension=0,
        tiled=True,
    ).astype(jnp.float32)
    small_here = final[:, mixer_width:].reshape(-1)
    small_out, at = [], 0
    for a in smalls:
        small_out.append(small_here[at : at + a.size].reshape(a.shape))
        at += a.size
    return (
        block_out,
        grad_in,
        small_out[0],
        final[:, : cuts[0]],
        final[:, cuts[0] : cuts[1]],
        final[:, cuts[1] : cuts[2]],
        final[:, cuts[2] : mixer_width],
        small_out[2],
        small_out[3],
        small_out[4],
        small_out[5],
        late[:, 2 * hidden_width : 2 * hidden_width + out_width].T,
        small_out[1],
        late[:, :hidden_width],
        late[:, hidden_width : 2 * hidden_width],
        late[:, 2 * hidden_width + out_width :].T,
    )


def solution(mesh):
    return jax.shard_map(
        per_device,
        mesh=mesh,
        in_specs=(
            P(None, "seq", "tp"),
            P(None, "seq", "tp"),
            P(None, "seq", "tp"),
            P(None, "seq", "tp"),
            P("seq"),
            P("seq", "tp"),
            P("seq", "tp"),
            P("seq", "tp"),
            P("seq", "tp"),
            P(None, "tp", "seq"),
            P(None, "tp", "seq"),
            P(None, "tp", "seq"),
            P("tp", "seq"),
            P("tp", "seq"),
            P("seq"),
            P("seq", "tp"),
            P("seq", "tp"),
            P("tp", "seq"),
        ),
        out_specs=(
            P(None, "seq", "tp"),
            P(None, "seq", "tp"),
            P("seq"),
            P("seq", "tp"),
            P("seq", "tp"),
            P("seq", "tp"),
            P("seq", "tp"),
            P(None, "tp", "seq"),
            P(None, "tp", "seq"),
            P(None, "tp", "seq"),
            P("tp", "seq"),
            P("tp", "seq"),
            P("seq"),
            P("seq", "tp"),
            P("seq", "tp"),
            P("tp", "seq"),
        ),
        check_vma=False,
    )
```

```python
import jax
import jax.numpy as jnp
from jax import lax
from jax.sharding import PartitionSpec as P

D = 1024
DK = 128
DV = 256
CONV = 4
BLOCK = 64


PRECISE = lax.Precision.HIGHEST
SPLIT = lax.Precision.HIGH
EPSILON = 1e-06
LOG_TWO = 0.6931471805599453


def shifted(block, axis, distance):
    devices = range(lax.axis_size(axis))
    route = [(i - distance, i) for i in devices if i - distance in devices]
    return lax.ppermute(block, axis, route)


def before_me(joint, axis):
    size = lax.axis_size(axis)
    held = shifted(joint.astype(jnp.bfloat16), axis, 1).astype(jnp.float32)
    distance = 1
    while distance < size:
        last = 2 * distance >= size
        sent = held[..., DK:] if last else held
        got = shifted(sent.astype(jnp.bfloat16), axis, distance).astype(jnp.float32)
        moved = jnp.matmul(held[..., :DK], got, precision=PRECISE)
        if last:
            return held[..., DK:] + moved
        held = jnp.concatenate(
            [moved[..., :DK], held[..., DK:] + moved[..., DK:]], axis=-1
        )
        distance *= 2
    return held[..., DK:]


def later_maps(transition, axis):
    size = lax.axis_size(axis)
    held = shifted(transition.astype(jnp.bfloat16), axis, -1).astype(jnp.float32)
    maps = [held]
    distance = 1
    while 2 * distance < size:
        got = shifted(held.astype(jnp.bfloat16), axis, -distance).astype(jnp.float32)
        held = jnp.matmul(got, held, precision=PRECISE)
        maps.append(held)
        distance *= 2
    return maps


def after_me(d_start, maps, axis):
    size = lax.axis_size(axis)
    held = shifted(d_start.astype(jnp.bfloat16), axis, -1).astype(jnp.float32)
    distance = 1
    for step in maps:
        if distance >= size:
            break
        got = shifted(held.astype(jnp.bfloat16), axis, -distance).astype(jnp.float32)
        held = held + jnp.einsum("bhkj,bhkw->bhjw", step, got, precision=PRECISE)
        distance *= 2
    return held


def row_scale(values):
    return lax.rsqrt(jnp.mean(values * values, axis=-1, keepdims=True) + EPSILON)


def silu_slope(values):
    sigmoid = jax.nn.sigmoid(values)
    return sigmoid * (1.0 + values * (1.0 - sigmoid))


def norm_back(d_normed, inputs, scales, gains):
    weighted = d_normed * gains
    return scales * (
        weighted - inputs * scales * scales * jnp.mean(weighted * inputs, axis=-1, keepdims=True)
    )


@jax.custom_vjp
def unit_inverse(strict_part):
    width = strict_part.shape[-1]
    negated = -strict_part
    result = jnp.eye(width, dtype=strict_part.dtype) + negated
    for rounds in range(width.bit_length() - 2):
        negated = jnp.matmul(negated, negated, precision=PRECISE)
        result = result + jnp.matmul(result, negated, precision=PRECISE)
    return result


def unit_inverse_forward(strict_part):
    result = unit_inverse(strict_part)
    return result, result


def unit_inverse_backward(result, d_result):
    flipped = jnp.swapaxes(result, -1, -2)
    inner = jnp.matmul(d_result, flipped, precision=SPLIT)
    return (-jnp.matmul(flipped, inner, precision=SPLIT),)


unit_inverse.defvjp(unit_inverse_forward, unit_inverse_backward)


def delta_run(state_in, query, keys, values, log_decay, write_strength_rate):
    leading = query.shape[:-2]
    length = query.shape[-2]
    blocks = length // BLOCK
    axis_at = len(leading)

    def split_blocks(tensor):
        return tensor.reshape(leading + (blocks, BLOCK) + tensor.shape[axis_at + 1 :])

    query, keys, values, log_decay, rate = (
        split_blocks(a) for a in (query, keys, values, log_decay, write_strength_rate)
    )
    cumulative = jnp.cumsum(log_decay, axis=-1)
    locations = jnp.arange(BLOCK)
    strictly = (locations[:, None] > locations[None, :]).astype(state_in.dtype)
    up_to = locations[:, None] >= locations[None, :]
    spread = cumulative[..., :, None] - cumulative[..., None, :]
    factors = jnp.exp(jnp.where(up_to, spread, 0.0)) * up_to.astype(state_in.dtype)
    key_dots = jnp.einsum("...td,...sd->...ts", keys, keys, precision=SPLIT)
    inverse = unit_inverse(rate[..., :, None] * key_dots * factors * strictly)
    growth = jnp.exp(cumulative)
    written = jnp.matmul(inverse, rate[..., None] * values, precision=SPLIT)
    erased = jnp.matmul(inverse, (rate * growth)[..., None] * keys, precision=SPLIT)
    scores = jnp.einsum("...td,...sd->...ts", query, keys, precision=SPLIT) * factors
    grown = growth[..., None] * query
    final_log = cumulative[..., -1:]
    faded = keys * jnp.exp(final_log - cumulative)[..., None]
    kept = jnp.exp(final_log)[..., None]
    state, outputs = state_in, []
    for block in range(blocks):
        at = (slice(None),) * axis_at + (block,)
        update = written[at] - jnp.matmul(erased[at], state, precision=SPLIT)
        outputs.append(
            jnp.matmul(grown[at], state, precision=SPLIT)
            + jnp.matmul(scores[at], update, precision=SPLIT)
        )
        state = kept[at] * state + jnp.einsum(
            "...sd,...sw->...dw", faded[at], update, precision=SPLIT
        )
    outputs = jnp.concatenate(outputs, axis=axis_at)
    return (outputs, state)


def conv_valid(kernel, extended):
    length = extended.shape[1] - kernel.shape[0] + 1
    return sum(
        (
            kernel[offset] * extended[:, offset : offset + length]
            for offset in range(kernel.shape[0])
        )
    )


def heads_first(tensor, width):
    shaped = tensor.reshape(tensor.shape[0], tensor.shape[1], -1, width)
    return jnp.transpose(shaped, (0, 2, 1, 3))


def rows_last(tensor):
    shaped = jnp.transpose(tensor, (0, 2, 1, 3))
    return shaped.reshape(shaped.shape[0], shaped.shape[1], -1)


def activate(kern_query, kern_key, kern_value, ext_query, ext_key, ext_value):
    query = heads_first(jax.nn.silu(conv_valid(kern_query, ext_query)), DK)
    query = (
        query * lax.rsqrt(jnp.sum(query * query, axis=-1, keepdims=True) + EPSILON) * DK ** (-0.5)
    )
    keys = heads_first(jax.nn.silu(conv_valid(kern_key, ext_key)), DK)
    keys = keys * lax.rsqrt(jnp.sum(keys * keys, axis=-1, keepdims=True) + EPSILON)
    values = heads_first(jax.nn.silu(conv_valid(kern_value, ext_value)), DV)
    return (query, keys, values)


def gate_rates(decay_code, beta_code):
    log_decay = -0.5 * jnp.exp(-LOG_TWO * decay_code.astype(jnp.float32))
    write_strength_rate = (beta_code.astype(jnp.float32) + 1.0) / 8.0
    return (jnp.moveaxis(log_decay, 2, 1), jnp.moveaxis(write_strength_rate, 2, 1))


def fold_edge(tensor, incoming):
    margin = incoming.shape[1]
    return jnp.concatenate([tensor[:, :-margin], tensor[:, -margin:] + incoming], axis=1)


def per_device(
    block_in,
    out_grad,
    decay_code,
    beta_code,
    norm_gain,
    w_query,
    w_key,
    w_value,
    w_outgate,
    conv_query,
    conv_key,
    conv_value,
    head_gain,
    w_output,
    mlp_gain,
    w_gate,
    w_up,
    w_down,
):
    seq_count, tok_count, width_part = block_in.shape
    heads_here = decay_code.shape[2]
    ranks = lax.axis_size("seq")
    smalls = (norm_gain, mlp_gain, conv_query, conv_key, conv_value, head_gain)
    flat = jnp.concatenate([a.reshape(-1) for a in smalls])
    extra = -(-flat.shape[0] // norm_gain.shape[0])
    flat = jnp.pad(flat, (0, extra * norm_gain.shape[0] - flat.shape[0]))
    first = jnp.concatenate(
        [w_query, w_key, w_value, w_outgate, flat.reshape(norm_gain.shape[0], extra)], axis=1
    )
    widths = (w_query.shape[1], w_key.shape[1], w_value.shape[1], w_outgate.shape[1])
    mixer_width = sum(widths)
    first = lax.all_gather(first, "seq", axis=0, tiled=True)
    second = lax.all_gather(
        jnp.concatenate([w_gate, w_up, w_output.T, w_down.T], axis=1), "seq", axis=0, tiled=True
    )
    hidden_width = w_gate.shape[1]
    out_width = w_output.shape[0]
    full_mixer = first[:, :mixer_width]
    full_gate_up = second[:, : 2 * hidden_width]
    output_t = second[:, 2 * hidden_width : 2 * hidden_width + out_width]
    down_t = second[:, 2 * hidden_width + out_width :]
    gathered = first[:, mixer_width:].reshape(ranks, -1)
    parts, at = [], 0
    for a in smalls:
        parts.append(gathered[:, at : at + a.size].reshape((ranks,) + a.shape))
        at += a.size
    gain_one, gain_two = parts[0].reshape(-1), parts[1].reshape(-1)
    kern_query, kern_key, kern_value = (
        jnp.moveaxis(a, 0, 2).reshape(a.shape[1], a.shape[2], -1) for a in parts[2:5]
    )
    gain_head = jnp.moveaxis(parts[5], 0, 1).reshape(head_gain.shape[0], -1)
    gain_one = gain_one.astype(jnp.float32)
    gain_two = gain_two.astype(jnp.float32)
    gain_head = gain_head.astype(jnp.float32)[None, :, None, :]
    kernels = tuple(
        (
            kernel.astype(jnp.float32).reshape(CONV, -1)
            for kernel in (kern_query, kern_key, kern_value)
        )
    )
    input_full = lax.all_gather(block_in, "tp", axis=2, tiled=True)
    residual = input_full.astype(jnp.float32).reshape(-1, D)
    scale_one = row_scale(residual)
    normed = (residual * scale_one * gain_one).astype(jnp.bfloat16)
    projected = jnp.dot(normed, full_mixer, preferred_element_type=jnp.float32)
    cuts = (widths[0], widths[0] + widths[1], widths[0] + widths[1] + widths[2])
    proj_qkv = projected[:, : cuts[2]].reshape(seq_count, tok_count, -1)
    proj_outgate = projected[:, cuts[2] :]
    margin = CONV - 1
    before = shifted(proj_qkv[:, -margin:], "seq", 1)
    ext_qkv = jnp.concatenate([before, proj_qkv], axis=1)
    ext_query, ext_key, ext_value = (
        ext_qkv[..., : cuts[0]],
        ext_qkv[..., cuts[0] : cuts[1]],
        ext_qkv[..., cuts[1] :],
    )
    log_decay, write_strength_rate = gate_rates(decay_code, beta_code)
    eye_batch = jnp.broadcast_to(jnp.eye(DK, dtype=jnp.float32), (seq_count, heads_here, DK, DK))
    zero_state = jnp.zeros((seq_count, heads_here, DK, DV), jnp.float32)
    query, keys, values = activate(
        kernels[0], kernels[1], kernels[2], ext_query, ext_key, ext_value
    )
    start_joint = jnp.concatenate([eye_batch, zero_state], axis=-1)
    values_joint = jnp.concatenate(
        [jnp.zeros(values.shape[:-1] + (DK,), jnp.float32), values], axis=-1
    )
    out_joint, end_joint = delta_run(
        start_joint, query, keys, values_joint, log_decay, write_strength_rate
    )
    transition = end_joint[..., :DK]
    start_state = before_me(end_joint, "seq")
    maps = later_maps(transition, "seq")
    start_map = out_joint[..., :DK]
    mixed = out_joint[..., DK:] + jnp.einsum(
        "bhtk,bhkw->bhtw", start_map, start_state, precision=PRECISE
    )
    head_scale = row_scale(mixed)
    head_out = mixed * head_scale * gain_head
    gate_pre = heads_first(proj_outgate.reshape(seq_count, tok_count, -1), DV)
    gated = (
        rows_last(head_out * jax.nn.silu(gate_pre))
        .reshape(seq_count * tok_count, -1)
        .astype(jnp.bfloat16)
    )
    attn_part = jnp.einsum("tk,nk->tn", gated, output_t, preferred_element_type=jnp.float32)
    attn = lax.psum(attn_part.astype(jnp.bfloat16), "tp").astype(jnp.float32)
    middle = residual + attn
    tp_at = lax.axis_index("tp") * width_part
    mid_part = lax.dynamic_slice_in_dim(middle, tp_at, width_part, 1).reshape(
        seq_count, tok_count, width_part
    )
    scale_two = row_scale(middle)
    normed_two = (middle * scale_two * gain_two).astype(jnp.bfloat16)
    pre_both = jnp.dot(normed_two, full_gate_up, preferred_element_type=jnp.float32)
    pre_gate, pre_up = pre_both[:, :hidden_width], pre_both[:, hidden_width:]
    hidden = (jax.nn.silu(pre_gate) * pre_up).astype(jnp.bfloat16)
    feedforward_portion = jnp.einsum(
        "tk,nk->tn", hidden, down_t, preferred_element_type=jnp.float32
    ).reshape(seq_count, tok_count, D)
    fed = lax.psum_scatter(
        feedforward_portion.astype(jnp.bfloat16), "tp", scatter_dimension=2, tiled=True
    )
    cot_full = lax.all_gather(out_grad, "tp", axis=2, tiled=True)
    cotangent = cot_full.reshape(-1, D)
    d_hidden = jnp.dot(cotangent, down_t, preferred_element_type=jnp.float32)
    grad_down_t = jnp.dot(cotangent.T, hidden, preferred_element_type=jnp.float32)
    d_pre_gate = (d_hidden * pre_up * silu_slope(pre_gate)).astype(jnp.bfloat16)
    d_pre_up = (d_hidden * jax.nn.silu(pre_gate)).astype(jnp.bfloat16)
    d_pre_both = jnp.concatenate([d_pre_gate, d_pre_up], axis=1)
    d_two_part = jnp.einsum(
        "tk,nk->tn", d_pre_both, full_gate_up, preferred_element_type=jnp.float32
    )
    d_normed_two = lax.psum(d_two_part.astype(jnp.bfloat16), "tp").astype(jnp.float32)
    grad_gate_up = jnp.dot(normed_two.T, d_pre_both, preferred_element_type=jnp.float32)
    grad_mlp_gain = jnp.sum(d_normed_two * middle * scale_two, axis=0)
    d_middle = cotangent.astype(jnp.float32) + norm_back(d_normed_two, middle, scale_two, gain_two)
    d_mid_low = d_middle.astype(jnp.bfloat16)
    d_gated = jnp.dot(d_mid_low, output_t, preferred_element_type=jnp.float32)
    grad_output_t = jnp.dot(d_mid_low.T, gated, preferred_element_type=jnp.float32)
    late = lax.psum_scatter(
        jnp.concatenate(
            [
                grad_gate_up.astype(jnp.bfloat16),
                grad_output_t.astype(jnp.bfloat16),
                grad_down_t.astype(jnp.bfloat16),
            ],
            axis=1,
        ),
        "seq",
        scatter_dimension=0,
        tiled=True,
    )
    d_gated_heads = heads_first(d_gated.reshape(seq_count, tok_count, -1), DV)
    d_outgate = (
        rows_last(d_gated_heads * head_out * silu_slope(gate_pre))
        .reshape(seq_count * tok_count, -1)
        .astype(jnp.bfloat16)
    )
    d_head = d_gated_heads * jax.nn.silu(gate_pre)
    grad_head_gain = jnp.sum(d_head * mixed * head_scale, axis=(0, 2))
    d_mixed = norm_back(d_head, mixed, head_scale, gain_head)
    d_start = jnp.einsum("bhtk,bhtw->bhkw", start_map, d_mixed, precision=PRECISE)
    d_end = after_me(d_start, maps, "seq")

    def mixer(kern_q, kern_k, kern_v, ext_q, ext_k, ext_v, start_in):
        query_in, keys_in, values_in = activate(kern_q, kern_k, kern_v, ext_q, ext_k, ext_v)
        return delta_run(start_in, query_in, keys_in, values_in, log_decay, write_strength_rate)

    mixer_out, mixer_back = jax.vjp(
        mixer, kernels[0], kernels[1], kernels[2], ext_query, ext_key, ext_value, start_state
    )
    totals = mixer_back((d_mixed, d_end))
    d_ext = jnp.concatenate([totals[3], totals[4], totals[5]], axis=-1)
    after = shifted(d_ext[:, :margin], "seq", -1)
    d_proj = fold_edge(d_ext[:, margin:], after).reshape(seq_count * tok_count, -1)
    d_proj = jnp.concatenate([d_proj.astype(jnp.bfloat16), d_outgate], axis=1)
    d_normed_part = jnp.einsum("tk,nk->tn", d_proj, full_mixer, preferred_element_type=jnp.float32)
    grad_mixer = jnp.dot(normed.T, d_proj, preferred_element_type=jnp.float32)
    d_normed_part, fed, late = lax.optimization_barrier((d_normed_part, fed, late))
    late = late.astype(jnp.float32)
    block_out = (mid_part + fed.astype(jnp.float32)).astype(jnp.bfloat16)
    d_normed = (
        lax.psum(d_normed_part.reshape(seq_count, tok_count, D).astype(jnp.bfloat16), "tp")
        .astype(jnp.float32)
        .reshape(-1, D)
    )
    grad_norm_gain = jnp.sum(d_normed * residual * scale_one, axis=0)
    grad_full = (d_middle + norm_back(d_normed, residual, scale_one, gain_one)).reshape(
        seq_count, tok_count, D
    )
    grad_in = lax.dynamic_slice_in_dim(grad_full, lax.axis_index("tp") * width_part, width_part, 2)
    conv_grads = tuple(
        jnp.moveaxis(total.reshape(CONV, heads_here, ranks, -1), 2, 0).reshape(ranks, -1)
        for total in totals[:3]
    )
    small_grads = jnp.concatenate(
        [
            grad_norm_gain.reshape(ranks, -1),
            grad_mlp_gain.reshape(ranks, -1),
            *conv_grads,
            jnp.moveaxis(grad_head_gain.reshape(heads_here, ranks, -1), 1, 0).reshape(ranks, -1),
        ],
        axis=1,
    )
    small_grads = jnp.pad(
        small_grads, ((0, 0), (0, extra * norm_gain.shape[0] - small_grads.shape[1]))
    ).reshape(ranks * norm_gain.shape[0], extra)
    final = lax.psum_scatter(
        jnp.concatenate(
            [grad_mixer.astype(jnp.bfloat16), small_grads.astype(jnp.bfloat16)], axis=1
        ),
        "seq",
        scatter_dimension=0,
        tiled=True,
    ).astype(jnp.float32)
    small_here = final[:, mixer_width:].reshape(-1)
    small_out, at = [], 0
    for a in smalls:
        small_out.append(small_here[at : at + a.size].reshape(a.shape))
        at += a.size
    return (
        block_out,
        grad_in,
        small_out[0],
        final[:, : cuts[0]],
        final[:, cuts[0] : cuts[1]],
        final[:, cuts[1] : cuts[2]],
        final[:, cuts[2] : mixer_width],
        small_out[2],
        small_out[3],
        small_out[4],
        small_out[5],
        late[:, 2 * hidden_width : 2 * hidden_width + out_width].T,
        small_out[1],
        late[:, :hidden_width],
        late[:, hidden_width : 2 * hidden_width],
        late[:, 2 * hidden_width + out_width :].T,
    )


def solution(mesh):
    return jax.shard_map(
        per_device,
        mesh=mesh,
        in_specs=(
            P(None, "seq", "tp"),
            P(None, "seq", "tp"),
            P(None, "seq", "tp"),
            P(None, "seq", "tp"),
            P("seq"),
            P("seq", "tp"),
            P("seq", "tp"),
            P("seq", "tp"),
            P("seq", "tp"),
            P(None, "tp", "seq"),
            P(None, "tp", "seq"),
            P(None, "tp", "seq"),
            P("tp", "seq"),
            P("tp", "seq"),
            P("seq"),
            P("seq", "tp"),
            P("seq", "tp"),
            P("tp", "seq"),
        ),
        out_specs=(
            P(None, "seq", "tp"),
            P(None, "seq", "tp"),
            P("seq"),
            P("seq", "tp"),
            P("seq", "tp"),
            P("seq", "tp"),
            P("seq", "tp"),
            P(None, "tp", "seq"),
            P(None, "tp", "seq"),
            P(None, "tp", "seq"),
            P("tp", "seq"),
            P("tp", "seq"),
            P("seq"),
            P("seq", "tp"),
            P("seq", "tp"),
            P("tp", "seq"),
        ),
        check_vma=False,
    )
```
